256 devices in a mesh: cells: 64 (over y, z, core), members: 4 (over x).
Axes of the slice: x: 4, y: 4, z: 8, core: 2. Of those that a mesh axis runs over, the one named last changes fastest.
Arguments:
- tmax: float32 [16, 97, 262144], P('members', None, 'cells'), may hold values from -24 to 24
- threshold: int32 [262144], P('cells'), may hold values from 0 to 79
- land_mask: int32 [262144], P('cells'), may hold values from 0 to 1, as said below
- region_id: int32 [262144], P('cells'), may hold values from 0 to 45, as said below
- block_fill: int32 [2048], P('cells'), may hold values from 64 to 128
- cell_area: float32 [262144], P('cells'), may hold values from 0.1 to 1
Outputs:
- region_index: float32 [16, 92, 46], P('members')
- cell_mean: float32 [92, 262144], P('members', 'cells')
- land_count: int32 [46], replicated
The draws below stay inside these ranges and needn't reach their ends.
Inputs may be any that keep to these rules, and one draw needn't show every extreme that they name: `land_mask`: in every block of 128 slots the first 46 slots are land. `region_id`: in every block of 128 slots the first 46 slots name every region once.
All inputs are finite; a program needn't handle non-finite values.
Results may differ from the reference program's by a relative error of at most 0.0003.
Values sent between devices are 32-bit elements; how exact they have to be, the bound alone decides.
No kernel may reach another device: no remote copies, remote signals or barrier semaphores. Data moves between devices by JAX's collectives and lax.ppermute only.
A program may use at most 64 MiB of HBM per device.

```python
import math
import jax
import jax.numpy as jnp
from jax import lax

MEMBERS = 16
DAYS = 92
WINDOW = 6
INPUT_DAYS = 97
REGIONS = 46
BLOCK = 128
BLOCKS = 2048
CELLS = 262144


def draw_land_mask(key, part):
    index = jnp.arange(CELLS, dtype=jnp.int32)
    chance = 300 + 650 * index // CELLS
    rolls = jax.random.randint(jax.random.fold_in(key, 11), (CELLS,), 0, 1000)
    land = (rolls < chance).astype(jnp.int32)
    forced = (index % BLOCK < REGIONS).astype(jnp.int32)
    return jnp.maximum(land, forced)


def draw_region_id(key, part):
    index = jnp.arange(CELLS, dtype=jnp.int32)
    position = index % BLOCK
    shifts = jax.random.randint(jax.random.fold_in(key, 21), (BLOCKS,), 0, REGIONS)
    shift = jnp.repeat(shifts, BLOCK)
    covered = (position + shift) % REGIONS
    loose = jax.random.randint(jax.random.fold_in(key, 22), (CELLS,), 0, REGIONS)
    return jnp.where(position < REGIONS, covered, loose).astype(jnp.int32)


def place_ends(values, stream_key, smallest, top_value):
    extent = values.shape
    spot = [jax.random.randint(jax.random.fold_in(stream_key, axis), (), 0, extent[axis]) for axis in range(len(extent))]
    values = values.at[tuple(spot)].set(smallest)
    longest = extent.index(max(extent))
    spot[longest] = (spot[longest] + 1) % extent[longest]
    return values.at[tuple(spot)].set(top_value)


def block_levels(stream_key, dims, split, least, largest):
    def one(dim, shards_of):
        steps = jax.random.uniform(jax.random.fold_in(jax.random.fold_in(stream_key, 6), dim), (shards_of,), jnp.float32, least / len(split), largest / len(split))
        return jnp.repeat(jnp.exp(steps), dims[dim] // shards_of).reshape((-1,) + (1,) * (len(dims) - dim - 1))

    factor_of = one(*split[0])
    for cut in split[1:]:
        factor_of = factor_of * one(*cut)
    return factor_of


def noise(own_key, extent, spread, bound, split=(), held_as=jnp.bfloat16):
    values = spread * jax.random.normal(own_key, extent, jnp.float32)
    if split:
        values = values * block_levels(own_key, extent, split, -0.22, 0.18)
    return jnp.clip(values, -bound, bound).astype(held_as)


def setup_inputs(seed: int = 0) -> dict:
    seeds = jax.random.split(jax.random.key(seed), 7)
    tmax = noise(seeds[0], (MEMBERS, INPUT_DAYS, CELLS), 4.0, 24.0, ((0, 4), (2, 64)), jnp.float32)
    threshold = place_ends(jax.random.randint(seeds[1], (CELLS,), 0, 80), jax.random.fold_in(seeds[1], 1), 0, 79).astype(jnp.int32)
    land_mask = draw_land_mask(jax.random.fold_in(seeds[6], 71), 0)
    region_id = draw_region_id(jax.random.fold_in(seeds[6], 71), 0)
    block_fill = place_ends(jax.random.randint(seeds[4], (BLOCKS,), BLOCK // 2, BLOCK + 1), jax.random.fold_in(seeds[4], 1), BLOCK // 2, BLOCK).astype(jnp.int32)
    cell_area = jnp.clip(jnp.exp(math.log(1.0) - 2.3025851 * jax.random.uniform(seeds[5], (CELLS,), jnp.float32) ** block_levels(seeds[5], (CELLS,), ((0, 64),), -0.2, 0.2)), 0.1, 1.0)
    return dict(tmax=tmax, threshold=threshold, land_mask=land_mask, region_id=region_id, block_fill=block_fill, cell_area=cell_area)


def reference(tmax, threshold, land_mask, region_id, block_fill, cell_area):
    position = jnp.arange(CELLS, dtype=jnp.int32) % BLOCK
    filled = jnp.repeat(block_fill, BLOCK)
    live = land_mask * (position < filled).astype(jnp.int32)
    weight = cell_area * live.astype(jnp.float32)
    matches = region_id[:, None] == jnp.arange(REGIONS, dtype=jnp.int32)[None, :]
    onehot = matches.astype(jnp.float32)
    area_sum = jnp.dot(weight, onehot, precision=lax.Precision.HIGHEST)
    land_count = jnp.sum(live[:, None] * matches.astype(jnp.int32), axis=0)
    limit = threshold.astype(jnp.float32) * 0.1

    def one_member(total, member):
        excess = jnp.maximum(member - limit[None, :], 0.0)
        rolled = excess[0:DAYS]
        for shift in range(1, WINDOW):
            rolled = rolled + excess[shift:shift + DAYS]
        rolled = rolled / WINDOW
        sums = jnp.dot(rolled * weight[None, :], onehot, precision=lax.Precision.HIGHEST)
        return total + rolled, sums / area_sum[None, :]

    start = jnp.zeros((DAYS, CELLS), jnp.float32)
    total, region_index = lax.scan(one_member, start, tmax)
    cell_mean = live.astype(jnp.float32)[None, :] * total / MEMBERS
    return region_index, cell_mean, land_count
```

```python
import jax
import jax.numpy as jnp
from jax import lax
from jax.experimental import pallas as pl
from jax.experimental.pallas import tpu as pltpu
from jax.sharding import Mesh, PartitionSpec as P

WINDOW = 6
REGIONS = 46
HALF = 64
CELL_AXES = ("y", "z", "core")


def fold_kernel(
    fill_ref, x_ref, thr_ref, mask_ref, rid_ref, area_ref,
    own_ref, up_ref, far_ref, down_ref, sums_ref, acc_ref, total_ref,
):
    step = pl.program_id(0)
    days_in = x_ref.shape[0]
    tiles = thr_ref.shape[0]
    members = x_ref.shape[1] // tiles
    block_days = own_ref.shape[0]
    lanes = thr_ref.shape[1]

    sub = lax.broadcasted_iota(jnp.int32, (tiles, lanes), 0)
    lane = lax.broadcasted_iota(jnp.int32, (tiles, lanes), 1)
    fill = jnp.zeros((tiles, lanes), jnp.int32)
    for r in range(tiles):
        fill = jnp.where(sub == r, fill_ref[step * tiles + r], fill)
    live = jnp.where(lane < fill, mask_ref[...], 0).astype(jnp.float32)
    weight = area_ref[...] * live
    limit = thr_ref[...].astype(jnp.float32) * 0.1

    total = None
    for m in range(members):
        one = jnp.maximum(x_ref[:, pl.ds(m, tiles, stride=members), :] - limit[None], 0.0)
        total = one if total is None else total + one
    total_ref[...] = total
    me = lax.axis_index("x")
    parts = 4
    scale = live * (1.0 / (WINDOW * members * parts))
    for k, out in enumerate((own_ref, up_ref, far_ref, down_ref)):
        first = lax.rem(me + k, parts) * block_days
        s = total_ref[pl.ds(first, block_days + WINDOW - 1)]
        pair = s[:-1] + s[1:]
        rolled = pair[0:block_days] + pair[2 : 2 + block_days] + pair[4 : 4 + block_days]
        out[...] = rolled * scale[None]

    group = 2 * members
    region = lax.broadcasted_iota(jnp.int32, (HALF, lanes), 0)
    part = None
    for pair in range(0, tiles // 2, 2):
        lefts, rights = [], []
        for p in (pair, pair + 1):
            def spread(v):
                rows = [jnp.broadcast_to(v[t : t + 1], (members, lanes)) for t in (2 * p, 2 * p + 1)]
                return jnp.concatenate(rows, axis=0)
            w8, l8, t8 = spread(weight), spread(live), spread(limit)
            x = x_ref[:, p * group : (p + 1) * group, :]
            e = jnp.maximum(x - t8[None], 0.0) * w8[None]
            e = e.reshape(days_in * group, lanes)
            lefts.append(jnp.concatenate([e, w8, l8], axis=0))
            hot = [
                (region == rid_ref[t : t + 1, :]).astype(jnp.float32) for t in (2 * p, 2 * p + 1)
            ]
            rights.append(jnp.concatenate(hot, axis=0))
        left = jnp.concatenate(lefts, axis=1)
        right = jnp.concatenate(rights, axis=1).astype(jnp.bfloat16)
        high = left.astype(jnp.bfloat16)
        low = (left - high.astype(jnp.float32)).astype(jnp.bfloat16)
        dims = (((1,), (1,)), ((), ()))
        both = lax.dot_general(high, right, dims, preferred_element_type=jnp.float32)
        both = both + lax.dot_general(low, right, dims, preferred_element_type=jnp.float32)
        part = both if part is None else part + both

    @pl.when(step == 0)
    def _():
        acc_ref[...] = part

    @pl.when(step > 0)
    def _():
        acc_ref[...] += part

    @pl.when(step == pl.num_programs(0) - 1)
    def _():
        days = days_in - WINDOW + 1
        v = acc_ref[...].reshape(days_in + 2, group, 2 * HALF)
        pair = v[: days_in - 1] + v[1:days_in]
        rolled = (pair[0:days] + pair[2 : 2 + days] + pair[4 : 4 + days]) * (1.0 / WINDOW)
        slots = sums_ref.shape[0]
        pad = jnp.zeros((4 * slots - days - 2, group, 2 * HALF), jnp.float32)
        v = jnp.concatenate([rolled, v[days_in:], pad], axis=0)
        s = v + pltpu.roll(pltpu.roll(v, members, 1), HALF, 2)
        r = pltpu.roll(s, HALF, 2)
        top = lax.broadcasted_iota(jnp.int32, (slots, group, 2 * HALF), 1) < members
        low = lax.broadcasted_iota(jnp.int32, (slots, group, 2 * HALF), 2) < HALF
        upper = jnp.where(low, s[0:slots], r[slots : 2 * slots])
        lower = jnp.where(low, r[2 * slots : 3 * slots], s[3 * slots :])
        sums_ref[...] = jnp.where(top, upper, lower)


def fold(x, thr, mask, rid, fill, area):
    days_in, rows, lanes = x.shape
    tiles = thr.shape[0]
    members = rows // tiles
    days = days_in - WINDOW + 1
    block_days = days // 4
    step_tiles = 8
    slots = 24
    flat = pl.BlockSpec((step_tiles, lanes), lambda i: (i, 0))
    block = jax.ShapeDtypeStruct((block_days, tiles, lanes), jnp.float32)
    return pl.pallas_call(
        fold_kernel,
        grid=(tiles // step_tiles,),
        in_specs=[
            pl.BlockSpec(memory_space=pltpu.SMEM),
            pl.BlockSpec((days_in, step_tiles * members, lanes), lambda i: (0, i, 0)),
            flat, flat, flat, flat,
        ],
        out_specs=[pl.BlockSpec((block_days, step_tiles, lanes), lambda i: (0, i, 0))] * 4
        + [pl.BlockSpec((slots, 2 * members, 2 * HALF), lambda i: (0, 0, 0))],
        out_shape=[block] * 4
        + [jax.ShapeDtypeStruct((slots, 2 * members, 2 * HALF), jnp.float32)],
        scratch_shapes=[
            pltpu.VMEM(((days_in + 2) * 2 * members, 2 * HALF), jnp.float32),
            pltpu.VMEM((days_in, step_tiles, lanes), jnp.float32),
        ],
        compiler_params=pltpu.CompilerParams(vmem_limit_bytes=40 * 1024 * 1024),
    )(fill, pltpu.with_memory_space_constraint(x, pltpu.HBM), thr, mask, rid, area)


def moved(array, axis, shift):
    size = lax.axis_size(axis)
    return lax.ppermute(array, axis, [(i, (i + shift) % size) for i in range(size)])


def sum_over_cells(sums, arrived):
    core = lax.axis_index("core")
    halves = sums.reshape(2, -1, *sums.shape[1:])
    mine = lax.dynamic_index_in_dim(halves, core, 0, False)
    other = lax.dynamic_index_in_dim(halves, 1 - core, 0, False)
    mine = mine + moved(other, "core", 1)
    mine = mine + moved(mine, "y", 1) + moved(mine, "y", 2) + moved(mine, "y", 3)
    above, below = moved(mine, "z", 7), moved(mine, "z", 1)
    two = mine + above
    three = two + below
    mine = three + moved(three, "z", 5) + moved(two, "z", 3)
    mine, arrived = lax.optimization_barrier((mine, arrived))
    other = moved(mine, "core", 1)
    first = jnp.where(core == 0, mine, other)
    second = jnp.where(core == 0, other, mine)
    return jnp.concatenate([first, second]), arrived


def shards(tmax, threshold, land_mask, region_id, block_fill, cell_area):
    members, days_in, cells = tmax.shape
    blocks = block_fill.shape[0]
    lanes = cells // blocks
    days = days_in - WINDOW + 1
    x = tmax.reshape(members, days_in, blocks, lanes).transpose(1, 2, 0, 3)
    x = x.reshape(days_in, blocks * members, lanes)
    tile = lambda a: a.reshape(blocks, lanes)
    own, up, far, down, sums = fold(
        x, tile(threshold), tile(land_mask), tile(region_id), block_fill, tile(cell_area)
    )
    arrived = (moved(up, "x", 1), moved(far, "x", 2), moved(down, "x", 3))
    sums, arrived = sum_over_cells(sums, arrived)
    cell_mean = (own + arrived[0] + arrived[1] + arrived[2]).reshape(-1, cells)
    slots = sums.shape[0]
    table = sums.reshape(slots, 2, members, 2, HALF).transpose(2, 1, 3, 0, 4)
    table = table.reshape(members, 4 * slots, HALF)[:, :, :REGIONS]
    region_index = table[:, :days] / table[:, days : days + 1]
    land_count = table[0, days + 1].astype(jnp.int32)
    return region_index, cell_mean, land_count


def solution(mesh):
    devices = mesh.devices.reshape(4, 8, 2, 4)
    fine = Mesh(devices, ("y", "z", "core", "x"))
    cells = P(CELL_AXES)
    return jax.shard_map(
        shards,
        mesh=fine,
        in_specs=(P("x", None, CELL_AXES), cells, cells, cells, cells, cells),
        out_specs=(P("x", None, None), P("x", CELL_AXES), P()),
        check_vma=False,
    )
```

```python
import jax
import jax.numpy as jnp
from jax import lax
from jax.experimental import pallas as pl
from jax.experimental.pallas import tpu as pltpu
from jax.sharding import Mesh, PartitionSpec as P

WINDOW = 6
REGIONS = 46
HALF = 64
PARTS = 4
SLOTS = 24
TILES = 8
CELL_AXES = ("y", "z", "core")


def live_cells(fill_ref, mask_ref, step):
    tiles, lanes = mask_ref.shape
    sub = lax.broadcasted_iota(jnp.int32, (tiles, lanes), 0)
    lane = lax.broadcasted_iota(jnp.int32, (tiles, lanes), 1)
    fill = jnp.zeros((tiles, lanes), jnp.int32)
    for r in range(tiles):
        fill = jnp.where(sub == r, fill_ref[step * tiles + r], fill)
    return jnp.where(lane < fill, mask_ref[...], 0).astype(jnp.float32)


def cell_sums(step, x_ref, live, limit, outs, total_ref):
    tiles, lanes = live.shape
    members = x_ref.shape[1] // tiles
    block_days = outs[0].shape[0]
    total = None
    for m in range(members):
        one = jnp.maximum(x_ref[:, pl.ds(m, tiles, stride=members), :] - limit[None], 0.0)
        total = one if total is None else total + one
    total_ref[...] = total
    me = lax.axis_index("x")
    scale = live * (1.0 / (WINDOW * members * PARTS))
    early = (2 * step < pl.num_programs(0)).astype(jnp.int32)
    ahead = (0, 1 + early, 2 + early, 3 - 2 * early)
    for k, out in zip(ahead, outs):
        first = lax.rem(me + k, PARTS) * block_days
        s = total_ref[pl.ds(first, block_days + WINDOW - 1)]
        pair = s[:-1] + s[1:]
        rolled = pair[0:block_days] + pair[2 : 2 + block_days] + pair[4 : 4 + block_days]
        out[...] = rolled * scale[None]


def region_sums(step, x_ref, live, weight, limit, rid_ref, sums_ref, acc_ref):
    days_in = x_ref.shape[0]
    tiles, lanes = live.shape
    members = x_ref.shape[1] // tiles
    group = 2 * members
    region = lax.broadcasted_iota(jnp.int32, (HALF, lanes), 0)

    def spread(v, t):
        rows = [jnp.broadcast_to(v[r : r + 1], (members, lanes)) for r in (t, t + 1)]
        return jnp.concatenate(rows, axis=0)

    part = None
    for pair in range(0, tiles // 2, 2):
        lefts, rights = [], []
        for p in (pair, pair + 1):
            w8, l8, t8 = spread(weight, 2 * p), spread(live, 2 * p), spread(limit, 2 * p)
            x = x_ref[:, p * group : (p + 1) * group, :]
            e = jnp.maximum(x - t8[None], 0.0) * w8[None]
            e = e.reshape(days_in * group, lanes)
            lefts.append(jnp.concatenate([e, w8, l8], axis=0))
            hot = [
                (region == rid_ref[t : t + 1, :]).astype(jnp.float32) for t in (2 * p, 2 * p + 1)
            ]
            rights.append(jnp.concatenate(hot, axis=0))
        left = jnp.concatenate(lefts, axis=1)
        right = jnp.concatenate(rights, axis=1).astype(jnp.bfloat16)
        high = left.astype(jnp.bfloat16)
        low = (left - high.astype(jnp.float32)).astype(jnp.bfloat16)
        dims = (((1,), (1,)), ((), ()))
        both = lax.dot_general(high, right, dims, preferred_element_type=jnp.float32)
        both = both + lax.dot_general(low, right, dims, preferred_element_type=jnp.float32)
        part = both if part is None else part + both

    @pl.when(step == 0)
    def _():
        acc_ref[...] = part

    @pl.when(step > 0)
    def _():
        acc_ref[...] += part

    @pl.when(step == pl.num_programs(0) - 1)
    def _():
        days = days_in - WINDOW + 1
        v = acc_ref[...].reshape(days_in + 2, group, 2 * HALF)
        pair = v[: days_in - 1] + v[1:days_in]
        rolled = (pair[0:days] + pair[2 : 2 + days] + pair[4 : 4 + days]) * (1.0 / WINDOW)
        pad = jnp.zeros((4 * SLOTS - days - 2, group, 2 * HALF), jnp.float32)
        v = jnp.concatenate([rolled, v[days_in:], pad], axis=0)
        s = v + pltpu.roll(pltpu.roll(v, members, 1), HALF, 2)
        r = pltpu.roll(s, HALF, 2)
        top = lax.broadcasted_iota(jnp.int32, (SLOTS, group, 2 * HALF), 1) < members
        low = lax.broadcasted_iota(jnp.int32, (SLOTS, group, 2 * HALF), 2) < HALF
        upper = jnp.where(low, s[0:SLOTS], r[SLOTS : 2 * SLOTS])
        lower = jnp.where(low, r[2 * SLOTS : 3 * SLOTS], s[3 * SLOTS :])
        sums_ref[...] = jnp.where(top, upper, lower)


def fold_kernel(fill_ref, x_ref, thr_ref, mask_ref, rid_ref, area_ref, *refs):
    *outs, sums_ref, acc_ref, total_ref = refs
    step = pl.program_id(0)
    live = live_cells(fill_ref, mask_ref, step)
    limit = thr_ref[...].astype(jnp.float32) * 0.1
    cell_sums(step, x_ref, live, limit, outs, total_ref)
    region_sums(step, x_ref, live, area_ref[...] * live, limit, rid_ref, sums_ref, acc_ref)


def table_kernel(mine_ref, other_ref, index_ref, count_ref, rows_ref):
    half, group, lanes = mine_ref.shape
    members = group // 2
    days = index_ref.shape[2]
    core = lax.axis_index("core")
    mine = mine_ref[...].reshape(half * group, lanes)
    other = other_ref[...].reshape(half * group, lanes)
    rows_ref[: half * group] = jnp.where(core == 0, mine, other)
    rows_ref[half * group :] = jnp.where(core == 0, other, mine)
    for m in range(members):
        upper = rows_ref[pl.ds(m, 2 * half, stride=group), :]
        lower = rows_ref[pl.ds(members + m, 2 * half, stride=group), :]
        rows = [upper, pltpu.roll(upper, HALF, 1), lower, pltpu.roll(lower, HALF, 1)]
        table = jnp.concatenate(rows, axis=0)
        if m == 0:
            count_ref[...] = table[days + 1 : days + 2, :REGIONS].astype(jnp.int32)
        by_region = table.T[:REGIONS]
        index_ref[:, m, :] = by_region[:, :days] / by_region[:, days : days + 1]


def call(kernel, fill, x, flats, blocks, regional):
    days_in, rows, lanes = x.shape
    tiles = flats[0].shape[0]
    members = rows // tiles
    block_days = (days_in - WINDOW + 1) // PARTS
    flat = pl.BlockSpec((TILES, lanes), lambda i: (i, 0))
    out_specs = [pl.BlockSpec((block_days, TILES, lanes), lambda i: (0, i, 0))] * blocks
    out_shape = [jax.ShapeDtypeStruct((block_days, tiles, lanes), jnp.float32)] * blocks
    scratch = []
    if regional:
        sums = (SLOTS, 2 * members, 2 * HALF)
        out_specs.append(pl.BlockSpec(sums, lambda i: (0, 0, 0)))
        out_shape.append(jax.ShapeDtypeStruct(sums, jnp.float32))
        scratch.append(pltpu.VMEM(((days_in + 2) * 2 * members, 2 * HALF), jnp.float32))
    if blocks:
        scratch.append(pltpu.VMEM((days_in, TILES, lanes), jnp.float32))
    return pl.pallas_call(
        kernel,
        grid=(tiles // TILES,),
        in_specs=[
            pl.BlockSpec(memory_space=pltpu.SMEM),
            pl.BlockSpec((days_in, TILES * members, lanes), lambda i: (0, i, 0)),
        ]
        + [flat] * len(flats),
        out_specs=out_specs,
        out_shape=out_shape,
        scratch_shapes=scratch,
        compiler_params=pltpu.CompilerParams(vmem_limit_bytes=40 * 1024 * 1024),
    )(*[pltpu.with_memory_space_constraint(a, pltpu.HBM) if a is not fill else a for a in (fill, x, *flats)])


def moved(array, axis, shift):
    size = lax.axis_size(axis)
    return lax.ppermute(array, axis, [(i, (i + shift) % size) for i in range(size)])


def sum_over_cells(sums):
    core = lax.axis_index("core")
    halves = sums.reshape(2, -1, *sums.shape[1:])
    mine = lax.dynamic_index_in_dim(halves, core, 0, False)
    other = lax.dynamic_index_in_dim(halves, 1 - core, 0, False)
    mine = mine + moved(other, "core", 1)
    mine = mine + moved(mine, "y", 1) + moved(mine, "y", 2) + moved(mine, "y", 3)
    two = mine + moved(mine, "z", 7)
    three = two + moved(mine, "z", 1)
    mine = three + moved(three, "z", 5) + moved(two, "z", 3)
    return mine, moved(mine, "core", 1)


def sum_over_members(own, up, down, late):
    tiles = own.shape[1]
    cut = tiles // 2
    from_below, from_above = moved(up, "x", 1), moved(down, "x", 3)
    near = moved(late[:, :cut] + from_below[:, :cut], "x", 1)
    far = moved(late[:, cut:] + from_above[:, cut:], "x", 3)
    first = own[:, :cut] + from_above[:, :cut] + near
    second = own[:, cut:] + from_below[:, cut:] + far
    return first, second


def shards(tmax, threshold, land_mask, region_id, block_fill, cell_area):
    members, days_in, cells = tmax.shape
    blocks = block_fill.shape[0]
    lanes = cells // blocks
    days = days_in - WINDOW + 1
    x = tmax.reshape(members, days_in, blocks, lanes).transpose(1, 2, 0, 3)
    x = x.reshape(days_in, blocks * members, lanes)
    threshold, land_mask, region_id, cell_area = (
        a.reshape(blocks, lanes) for a in (threshold, land_mask, region_id, cell_area)
    )
    *terms, sums = call(
        fold_kernel, block_fill, x, (threshold, land_mask, region_id, cell_area), PARTS, True
    )
    first, second = sum_over_members(*terms)
    mine, other = sum_over_cells(sums)
    cell_mean = jnp.concatenate([first, second], axis=1).reshape(-1, cells)
    region_index, land_count = pl.pallas_call(
        table_kernel,
        out_shape=[
            jax.ShapeDtypeStruct((REGIONS, members, days), jnp.float32),
            jax.ShapeDtypeStruct((1, REGIONS), jnp.int32),
        ],
        scratch_shapes=[pltpu.VMEM((SLOTS * 2 * members, 2 * HALF), jnp.float32)],
        compiler_params=pltpu.CompilerParams(vmem_limit_bytes=4 * 1024 * 1024),
    )(mine, other)
    return region_index.transpose(1, 2, 0), cell_mean, land_count.reshape(REGIONS)


def solution(mesh):
    devices = mesh.devices.reshape(4, 8, 2, 4)
    fine = Mesh(devices, ("y", "z", "core", "x"))
    cells = P(CELL_AXES)
    return jax.shard_map(
        shards,
        mesh=fine,
        in_specs=(P("x", None, CELL_AXES), cells, cells, cells, cells, cells),
        out_specs=(P("x", None, None), P("x", CELL_AXES), P()),
        check_vma=False,
    )
```

```python
import jax
import jax.numpy as jnp
from jax import lax
from jax.experimental import pallas as pl
from jax.experimental.pallas import tpu as pltpu
from jax.sharding import Mesh, PartitionSpec as P

WINDOW = 6
REGIONS = 46
HALF = 64
PARTS = 4
SLOTS = 24
TILES = 16
CHUNK = 8
CELL_AXES = ("y", "z", "core")


def live_cells(fill_ref, mask_ref, step):
    tiles, lanes = mask_ref.shape
    blocks = fill_ref.shape[1]
    row = lax.broadcasted_iota(jnp.int32, (tiles, blocks), 0) + step * tiles
    here = row == lax.broadcasted_iota(jnp.int32, (tiles, blocks), 1)
    fill = jnp.where(here, fill_ref[...].astype(jnp.float32), 0.0)
    fill = jnp.sum(fill, axis=1, keepdims=True).astype(jnp.int32)
    lane = lax.broadcasted_iota(jnp.int32, (tiles, lanes), 1)
    return jnp.where(lane < fill, mask_ref[...], 0).astype(jnp.float32)


def excess_terms(x_ref, weight, live, limit, excess_ref, left_ref):
    days_in = x_ref.shape[0]
    tiles, lanes = live.shape
    members = x_ref.shape[1] // tiles
    group = 2 * members
    width = tiles // 2 * lanes

    def spread(v, t):
        rows = [jnp.broadcast_to(v[r : r + 1], (members, lanes)) for r in (t, t + 1)]
        return jnp.concatenate(rows, axis=0)

    for p in range(tiles // 2):
        w8, l8, t8 = spread(weight, 2 * p), spread(live, 2 * p), spread(limit, 2 * p)

        def keep(first, v):
            high = v.astype(jnp.bfloat16)
            low = (v - high.astype(jnp.float32)).astype(jnp.bfloat16)
            left_ref[first : first + v.shape[0], p * lanes : (p + 1) * lanes] = high
            left_ref[first : first + v.shape[0], width + p * lanes : width + (p + 1) * lanes] = low

        for d in range(0, days_in, CHUNK):
            n = min(CHUNK, days_in - d)
            e = jnp.maximum(x_ref[d : d + n, p * group : (p + 1) * group, :] - t8[None], 0.0)
            excess_ref[d : d + n, p * group : (p + 1) * group, :] = e
            rows = (e * w8[None]).reshape(n * group, lanes)
            if d + n == days_in:
                rows = jnp.concatenate([rows, w8, l8, jnp.zeros((left_ref.shape[0] - (days_in + 2) * group, lanes), jnp.float32)], axis=0)
            keep(d * group, rows)


def cell_sums(step, excess_ref, live, outs, total_ref):
    days_in = excess_ref.shape[0]
    tiles, lanes = live.shape
    members = excess_ref.shape[1] // tiles
    block_days = outs[0].shape[0]
    for d in range(0, days_in, CHUNK):
        n = min(CHUNK, days_in - d)
        total = excess_ref[d : d + n, pl.ds(0, tiles, stride=members), :]
        for m in range(1, members):
            total = total + excess_ref[d : d + n, pl.ds(m, tiles, stride=members), :]
        total_ref[d : d + n] = total
    me = lax.axis_index("x")
    scale = live * (1.0 / (WINDOW * members * PARTS))
    early = (2 * step < pl.num_programs(0)).astype(jnp.int32)
    ahead = (0, 1 + early, 2 + early, 3 - 2 * early)
    for k, out in zip(ahead, outs):
        first = lax.rem(me + k, PARTS) * block_days
        s = total_ref[pl.ds(first, block_days + WINDOW - 1)]
        pair = s[:-1] + s[1:]
        rolled = pair[0:block_days] + pair[2 : 2 + block_days] + pair[4 : 4 + block_days]
        out[...] = rolled * scale[None]


def region_sums(step, left_ref, rid_ref, acc_ref):
    tiles, lanes = rid_ref.shape
    region = lax.broadcasted_iota(jnp.int32, (HALF, lanes), 0)

    def hot(t):
        return (region == rid_ref[t : t + 1, :]).astype(jnp.float32)

    even = jnp.concatenate([hot(t) for t in range(0, tiles, 2)], axis=1)
    odd = jnp.concatenate([hot(t) for t in range(1, tiles, 2)], axis=1)
    right = jnp.concatenate([even, odd], axis=0).astype(jnp.bfloat16)
    right = jnp.concatenate([right, right], axis=1)
    part = lax.dot_general(
        left_ref[...], right, (((1,), (1,)), ((), ())), preferred_element_type=jnp.float32
    )

    @pl.when(step == 0)
    def _():
        acc_ref[...] = part

    @pl.when(step > 0)
    def _():
        acc_ref[...] += part


def packed_sums(acc_ref, sums_ref, days_in):
    group = sums_ref.shape[1]
    members = group // 2
    days = days_in - WINDOW + 1
    v = acc_ref[: (days_in + 2) * group].reshape(days_in + 2, group, 2 * HALF)
    pair = v[: days_in - 1] + v[1:days_in]
    rolled = (pair[0:days] + pair[2 : 2 + days] + pair[4 : 4 + days]) * (1.0 / WINDOW)
    pad = jnp.zeros((4 * SLOTS - days - 2, group, 2 * HALF), jnp.float32)
    v = jnp.concatenate([rolled, v[days_in:], pad], axis=0)
    s = v + pltpu.roll(pltpu.roll(v, members, 1), HALF, 2)
    r = pltpu.roll(s, HALF, 2)
    top = lax.broadcasted_iota(jnp.int32, (SLOTS, group, 2 * HALF), 1) < members
    low = lax.broadcasted_iota(jnp.int32, (SLOTS, group, 2 * HALF), 2) < HALF
    upper = jnp.where(low, s[0:SLOTS], r[SLOTS : 2 * SLOTS])
    lower = jnp.where(low, r[2 * SLOTS : 3 * SLOTS], s[3 * SLOTS :])
    sums_ref[...] = jnp.where(top, upper, lower)


def fold_kernel(fill_ref, x_ref, thr_ref, mask_ref, rid_ref, area_ref, *refs):
    *outs, sums_ref, acc_ref, total_ref, excess_ref, left_ref = refs
    step = pl.program_id(0)
    live = live_cells(fill_ref, mask_ref, step)
    limit = thr_ref[...].astype(jnp.float32) * 0.1
    excess_terms(x_ref, area_ref[...] * live, live, limit, excess_ref, left_ref)
    region_sums(step, left_ref, rid_ref, acc_ref)
    cell_sums(step, excess_ref, live, outs, total_ref)

    @pl.when(step == pl.num_programs(0) - 1)
    def _():
        packed_sums(acc_ref, sums_ref, x_ref.shape[0])


def table_kernel(mine_ref, other_ref, index_ref, count_ref, rows_ref):
    half, group, lanes = mine_ref.shape
    members = group // 2
    days = index_ref.shape[2]
    core = lax.axis_index("core")
    mine = mine_ref[...].reshape(half * group, lanes)
    other = other_ref[...].reshape(half * group, lanes)
    rows_ref[: half * group] = jnp.where(core == 0, mine, other)
    rows_ref[half * group :] = jnp.where(core == 0, other, mine)
    for m in range(members):
        upper = rows_ref[pl.ds(m, 2 * half, stride=group), :]
        lower = rows_ref[pl.ds(members + m, 2 * half, stride=group), :]
        rows = [upper, pltpu.roll(upper, HALF, 1), lower, pltpu.roll(lower, HALF, 1)]
        table = jnp.concatenate(rows, axis=0)
        if m == 0:
            count_ref[...] = table[days + 1 : days + 2, :REGIONS].astype(jnp.int32)
        by_region = table.T[:REGIONS]
        index_ref[:, m, :] = by_region[:, :days] / by_region[:, days : days + 1]


def call(kernel, fill, x, flats, blocks, regional):
    days_in, rows, lanes = x.shape
    tiles = flats[0].shape[0]
    members = rows // tiles
    block_days = (days_in - WINDOW + 1) // PARTS
    flat = pl.BlockSpec((TILES, lanes), lambda i: (i, 0))
    out_specs = [pl.BlockSpec((block_days, TILES, lanes), lambda i: (0, i, 0))] * blocks
    out_shape = [jax.ShapeDtypeStruct((block_days, tiles, lanes), jnp.float32)] * blocks
    scratch = []
    if regional:
        sums = (SLOTS, 2 * members, 2 * HALF)
        out_specs.append(pl.BlockSpec(sums, lambda i: (0, 0, 0)))
        out_shape.append(jax.ShapeDtypeStruct(sums, jnp.float32))
        high = -(-(days_in + 2) * 2 * members // 16) * 16
        scratch = [
            pltpu.VMEM((high, 2 * HALF), jnp.float32),
            pltpu.VMEM((days_in, TILES, lanes), jnp.float32),
            pltpu.VMEM((days_in, TILES * members, lanes), jnp.float32),
            pltpu.VMEM((high, TILES * lanes), jnp.bfloat16),
        ]
    return pl.pallas_call(
        kernel,
        grid=(tiles // TILES,),
        in_specs=[
            pl.BlockSpec(fill.shape, lambda i: (0, 0)),
            pl.BlockSpec((days_in, TILES * members, lanes), lambda i: (0, i, 0)),
        ]
        + [flat] * len(flats),
        out_specs=out_specs,
        out_shape=out_shape,
        scratch_shapes=scratch,
        compiler_params=pltpu.CompilerParams(vmem_limit_bytes=40 * 1024 * 1024),
    )(*[pltpu.with_memory_space_constraint(a, pltpu.HBM) for a in (fill, x, *flats)])


def moved(array, axis, shift):
    size = lax.axis_size(axis)
    return lax.ppermute(array, axis, [(i, (i + shift) % size) for i in range(size)])


def sum_over_cells(sums):
    core = lax.axis_index("core")
    halves = sums.reshape(2, -1, *sums.shape[1:])
    mine = lax.dynamic_index_in_dim(halves, core, 0, False)
    other = lax.dynamic_index_in_dim(halves, 1 - core, 0, False)
    mine = mine + moved(other, "core", 1)
    mine = mine + moved(mine, "y", 1) + moved(mine, "y", 2) + moved(mine, "y", 3)
    two = mine + moved(mine, "z", 7)
    three = two + moved(mine, "z", 1)
    mine = three + moved(three, "z", 5) + moved(two, "z", 3)
    return mine, moved(mine, "core", 1)


def sum_over_members(own, up, down, late):
    tiles = own.shape[1]
    cut = tiles // 2
    from_below, from_above = moved(up, "x", 1), moved(down, "x", 3)
    near = moved(late[:, :cut] + from_below[:, :cut], "x", 1)
    far = moved(late[:, cut:] + from_above[:, cut:], "x", 3)
    first = own[:, :cut] + from_above[:, :cut] + near
    second = own[:, cut:] + from_below[:, cut:] + far
    return first, second


def shards(tmax, threshold, land_mask, region_id, block_fill, cell_area):
    members, days_in, cells = tmax.shape
    blocks = block_fill.shape[0]
    lanes = cells // blocks
    days = days_in - WINDOW + 1
    x = tmax.reshape(members, days_in, blocks, lanes).transpose(1, 2, 0, 3)
    x = x.reshape(days_in, blocks * members, lanes)
    threshold, land_mask, region_id, cell_area = (
        a.reshape(blocks, lanes) for a in (threshold, land_mask, region_id, cell_area)
    )
    *terms, sums = call(
        fold_kernel, block_fill.reshape(1, blocks), x, (threshold, land_mask, region_id, cell_area), PARTS, True
    )
    first, second = sum_over_members(*terms)
    mine, other = sum_over_cells(sums)
    cell_mean = jnp.concatenate([first, second], axis=1).reshape(-1, cells)
    region_index, land_count = pl.pallas_call(
        table_kernel,
        out_shape=[
            jax.ShapeDtypeStruct((REGIONS, members, days), jnp.float32),
            jax.ShapeDtypeStruct((1, REGIONS), jnp.int32),
        ],
        scratch_shapes=[pltpu.VMEM((SLOTS * 2 * members, 2 * HALF), jnp.float32)],
        compiler_params=pltpu.CompilerParams(vmem_limit_bytes=4 * 1024 * 1024),
    )(mine, other)
    return region_index.transpose(1, 2, 0), cell_mean, land_count.reshape(REGIONS)


def solution(mesh):
    devices = mesh.devices.reshape(4, 8, 2, 4)
    fine = Mesh(devices, ("y", "z", "core", "x"))
    cells = P(CELL_AXES)
    return jax.shard_map(
        shards,
        mesh=fine,
        in_specs=(P("x", None, CELL_AXES), cells, cells, cells, cells, cells),
        out_specs=(P("x", None, None), P("x", CELL_AXES), P()),
        check_vma=False,
    )
```

```python
import jax
import jax.numpy as jnp
from jax import lax
from jax.experimental import pallas as pl
from jax.experimental.pallas import tpu as pltpu
from jax.sharding import Mesh, PartitionSpec as P

WINDOW = 6
REGIONS = 46
HALF = 64
PARTS = 4
ROWS = 48
TILES = 16
CHUNK = 8
CELL_AXES = ("y", "z", "core")


def live_cells(fill_ref, mask_ref, step):
    tiles, lanes = mask_ref.shape
    blocks = fill_ref.shape[1]
    row = lax.broadcasted_iota(jnp.int32, (tiles, blocks), 0) + step * tiles
    here = row == lax.broadcasted_iota(jnp.int32, (tiles, blocks), 1)
    fill = jnp.where(here, fill_ref[...].astype(jnp.float32), 0.0)
    fill = jnp.sum(fill, axis=1, keepdims=True).astype(jnp.int32)
    lane = lax.broadcasted_iota(jnp.int32, (tiles, lanes), 1)
    return jnp.where(lane < fill, mask_ref[...], 0).astype(jnp.float32)


def excess_terms(x_ref, weight, live, limit, excess_ref, left_ref):
    days_in = x_ref.shape[0]
    tiles, lanes = live.shape
    members = x_ref.shape[1] // tiles
    group = 2 * members
    width = tiles // 2 * lanes

    def spread(v, t):
        rows = [jnp.broadcast_to(v[r : r + 1], (members, lanes)) for r in (t, t + 1)]
        return jnp.concatenate(rows, axis=0)

    for p in range(tiles // 2):
        w8, l8, t8 = spread(weight, 2 * p), spread(live, 2 * p), spread(limit, 2 * p)

        def keep(first, v):
            high = v.astype(jnp.bfloat16)
            low = (v - high.astype(jnp.float32)).astype(jnp.bfloat16)
            left_ref[first : first + v.shape[0], p * lanes : (p + 1) * lanes] = high
            left_ref[first : first + v.shape[0], width + p * lanes : width + (p + 1) * lanes] = low

        for d in range(0, days_in, CHUNK):
            n = min(CHUNK, days_in - d)
            e = jnp.maximum(x_ref[d : d + n, p * group : (p + 1) * group, :] - t8[None], 0.0)
            excess_ref[d : d + n, p * group : (p + 1) * group, :] = e
            rows = (e * w8[None]).reshape(n * group, lanes)
            if d + n == days_in:
                rows = jnp.concatenate([rows, w8, l8, jnp.zeros((left_ref.shape[0] - (days_in + 2) * group, lanes), jnp.float32)], axis=0)
            keep(d * group, rows)


def cell_sums(step, excess_ref, live, outs, total_ref):
    days_in = excess_ref.shape[0]
    tiles, lanes = live.shape
    members = excess_ref.shape[1] // tiles
    block_days = outs[0].shape[0]
    for d in range(0, days_in, CHUNK):
        n = min(CHUNK, days_in - d)
        total = excess_ref[d : d + n, pl.ds(0, tiles, stride=members), :]
        for m in range(1, members):
            total = total + excess_ref[d : d + n, pl.ds(m, tiles, stride=members), :]
        total_ref[d : d + n] = total
    me = lax.axis_index("x")
    scale = live * (1.0 / (WINDOW * members * PARTS))
    early = (2 * step < pl.num_programs(0)).astype(jnp.int32)
    ahead = (0, 1 + early, 2 + early, 3 - 2 * early)
    for k, out in zip(ahead, outs):
        first = lax.rem(me + k, PARTS) * block_days
        s = total_ref[pl.ds(first, block_days + WINDOW - 1)]
        pair = s[:-1] + s[1:]
        rolled = pair[0:block_days] + pair[2 : 2 + block_days] + pair[4 : 4 + block_days]
        out[...] = rolled * scale[None]


def region_sums(step, left_ref, rid_ref, acc_ref):
    tiles, lanes = rid_ref.shape
    region = lax.broadcasted_iota(jnp.int32, (HALF, lanes), 0)

    def hot(t):
        return (region == rid_ref[t : t + 1, :]).astype(jnp.float32)

    even = jnp.concatenate([hot(t) for t in range(0, tiles, 2)], axis=1)
    odd = jnp.concatenate([hot(t) for t in range(1, tiles, 2)], axis=1)
    right = jnp.concatenate([even, odd], axis=0).astype(jnp.bfloat16)
    right = jnp.concatenate([right, right], axis=1)
    part = lax.dot_general(
        left_ref[...], right, (((1,), (1,)), ((), ())), preferred_element_type=jnp.float32
    )

    @pl.when(step == 0)
    def _():
        acc_ref[...] = part

    @pl.when(step > 0)
    def _():
        acc_ref[...] += part


def packed_sums(acc_ref, sums_ref, days_in, members):
    group = 2 * members
    days = days_in - WINDOW + 1
    columns = sums_ref.shape[1] // members
    v = acc_ref[: (days_in + 2) * group].reshape(days_in + 2, group, 2 * HALF)
    pair = v[: days_in - 1] + v[1:days_in]
    rolled = (pair[0:days] + pair[2 : 2 + days] + pair[4 : 4 + days]) * (1.0 / WINDOW)
    acc_ref[: days * group] = rolled.reshape(days * group, 2 * HALF)
    acc_ref[days * group : (days + 2) * group] = v[days_in:].reshape(2 * group, 2 * HALF)
    rows = []
    for m in range(members):
        even = acc_ref[pl.ds(m, columns, stride=group), :]
        odd = acc_ref[pl.ds(members + m, columns, stride=group), :]
        rows.append(even + pltpu.roll(odd, HALF, 1))
    sums_ref[...] = jnp.concatenate(rows, axis=0).T[: sums_ref.shape[0]]


def fold_kernel(fill_ref, x_ref, thr_ref, mask_ref, rid_ref, area_ref, *refs):
    *outs, sums_ref, acc_ref, total_ref, excess_ref, left_ref = refs
    step = pl.program_id(0)
    live = live_cells(fill_ref, mask_ref, step)
    limit = thr_ref[...].astype(jnp.float32) * 0.1
    excess_terms(x_ref, area_ref[...] * live, live, limit, excess_ref, left_ref)
    region_sums(step, left_ref, rid_ref, acc_ref)
    cell_sums(step, excess_ref, live, outs, total_ref)

    @pl.when(step == pl.num_programs(0) - 1)
    def _():
        packed_sums(acc_ref, sums_ref, x_ref.shape[0], x_ref.shape[1] // live.shape[0])


def table_kernel(mine_ref, other_ref, index_ref, count_ref):
    members, days = index_ref.shape[1:]
    width = mine_ref.shape[1]
    columns = width // members
    first = lax.axis_index("core") == 0
    mine, other = mine_ref[...], other_ref[...]
    table = jnp.concatenate([jnp.where(first, mine, other), jnp.where(first, other, mine)], axis=0)
    count = jnp.broadcast_to(table[:, days + 1 : days + 2], (table.shape[0], 128)).T
    count_ref[...] = count[:1, :REGIONS].astype(jnp.int32)
    table = table / table[:, days : days + 1]
    for m in range(members):
        shifted = pltpu.roll(table, (width - m * columns) % width, 1) if m else table
        index_ref[:, m, :] = shifted[:REGIONS, :days]


def call(kernel, fill, x, flats, blocks, regional):
    days_in, rows, lanes = x.shape
    tiles = flats[0].shape[0]
    members = rows // tiles
    block_days = (days_in - WINDOW + 1) // PARTS
    flat = pl.BlockSpec((TILES, lanes), lambda i: (i, 0))
    out_specs = [pl.BlockSpec((block_days, TILES, lanes), lambda i: (0, i, 0))] * blocks
    out_shape = [jax.ShapeDtypeStruct((block_days, tiles, lanes), jnp.float32)] * blocks
    scratch = []
    if regional:
        columns = -(-(days_in - WINDOW + 3) // 8) * 8
        sums = (ROWS, members * columns)
        out_specs.append(pl.BlockSpec(sums, lambda i: (0, 0)))
        out_shape.append(jax.ShapeDtypeStruct(sums, jnp.float32))
        high = -(-(days_in + 2) * 2 * members // 16) * 16
        scratch = [
            pltpu.VMEM((high, 2 * HALF), jnp.float32),
            pltpu.VMEM((days_in, TILES, lanes), jnp.float32),
            pltpu.VMEM((days_in, TILES * members, lanes), jnp.float32),
            pltpu.VMEM((high, TILES * lanes), jnp.bfloat16),
        ]
    return pl.pallas_call(
        kernel,
        grid=(tiles // TILES,),
        in_specs=[
            pl.BlockSpec(fill.shape, lambda i: (0, 0)),
            pl.BlockSpec((days_in, TILES * members, lanes), lambda i: (0, i, 0)),
        ]
        + [flat] * len(flats),
        out_specs=out_specs,
        out_shape=out_shape,
        scratch_shapes=scratch,
        compiler_params=pltpu.CompilerParams(vmem_limit_bytes=40 * 1024 * 1024),
    )(*[pltpu.with_memory_space_constraint(a, pltpu.HBM) for a in (fill, x, *flats)])


def moved(array, axis, shift):
    size = lax.axis_size(axis)
    return lax.ppermute(array, axis, [(i, (i + shift) % size) for i in range(size)])


def sum_over_cells(sums):
    core = lax.axis_index("core")
    halves = sums.reshape(2, -1, *sums.shape[1:])
    mine = lax.dynamic_index_in_dim(halves, core, 0, False)
    other = lax.dynamic_index_in_dim(halves, 1 - core, 0, False)
    mine = mine + moved(other, "core", 1)
    mine = mine + moved(mine, "y", 1) + moved(mine, "y", 2) + moved(mine, "y", 3)
    two = mine + moved(mine, "z", 7)
    three = two + moved(mine, "z", 1)
    mine = three + moved(three, "z", 5) + moved(two, "z", 3)
    return mine, moved(mine, "core", 1)


def sum_over_members(own, up, down, late):
    tiles = own.shape[1]
    cut = tiles // 2
    from_below, from_above = moved(up, "x", 1), moved(down, "x", 3)
    near = moved(late[:, :cut] + from_below[:, :cut], "x", 1)
    far = moved(late[:, cut:] + from_above[:, cut:], "x", 3)
    first = own[:, :cut] + from_above[:, :cut] + near
    second = own[:, cut:] + from_below[:, cut:] + far
    return first, second


def shards(tmax, threshold, land_mask, region_id, block_fill, cell_area):
    members, days_in, cells = tmax.shape
    blocks = block_fill.shape[0]
    lanes = cells // blocks
    days = days_in - WINDOW + 1
    x = tmax.reshape(members, days_in, blocks, lanes).transpose(1, 2, 0, 3)
    x = x.reshape(days_in, blocks * members, lanes)
    threshold, land_mask, region_id, cell_area = (
        a.reshape(blocks, lanes) for a in (threshold, land_mask, region_id, cell_area)
    )
    *terms, sums = call(
        fold_kernel, block_fill.reshape(1, blocks), x, (threshold, land_mask, region_id, cell_area), PARTS, True
    )
    first, second = sum_over_members(*terms)
    mine, other = sum_over_cells(sums)
    cell_mean = jnp.concatenate([first, second], axis=1).reshape(-1, cells)
    other, cell_mean = lax.optimization_barrier((other, cell_mean))
    region_index, land_count = pl.pallas_call(
        table_kernel,
        out_shape=[
            jax.ShapeDtypeStruct((REGIONS, members, days), jnp.float32),
            jax.ShapeDtypeStruct((1, REGIONS), jnp.int32),
        ],
        compiler_params=pltpu.CompilerParams(vmem_limit_bytes=4 * 1024 * 1024),
    )(mine, other)
    return region_index.transpose(1, 2, 0), cell_mean, land_count.reshape(REGIONS)


def solution(mesh):
    devices = mesh.devices.reshape(4, 8, 2, 4)
    fine = Mesh(devices, ("y", "z", "core", "x"))
    cells = P(CELL_AXES)
    return jax.shard_map(
        shards,
        mesh=fine,
        in_specs=(P("x", None, CELL_AXES), cells, cells, cells, cells, cells),
        out_specs=(P("x", None, None), P("x", CELL_AXES), P()),
        check_vma=False,
    )
```

```python
import jax
import jax.numpy as jnp
from jax import lax
from jax.experimental import pallas as pl
from jax.experimental.pallas import tpu as pltpu
from jax.sharding import Mesh, PartitionSpec as P

WINDOW = 6
REGIONS = 46
HALF = 64
PARTS = 4
ROWS = 48
TILES = 16
CHUNK = 8
CELL_AXES = ("y", "z", "core")


def live_cells(fill_ref, mask_ref, step):
    tiles, lanes = mask_ref.shape
    blocks = fill_ref.shape[1]
    row = lax.broadcasted_iota(jnp.int32, (tiles, blocks), 0) + step * tiles
    here = row == lax.broadcasted_iota(jnp.int32, (tiles, blocks), 1)
    fill = jnp.where(here, fill_ref[...].astype(jnp.float32), 0.0)
    fill = jnp.sum(fill, axis=1, keepdims=True).astype(jnp.int32)
    lane = lax.broadcasted_iota(jnp.int32, (tiles, lanes), 1)
    return jnp.where(lane < fill, mask_ref[...], 0).astype(jnp.float32)


def excess_terms(x_ref, weight, live, limit, excess_ref, left_ref):
    days_in = x_ref.shape[0]
    tiles, lanes = live.shape
    members = x_ref.shape[1] // tiles
    group = 2 * members
    width = tiles // 2 * lanes

    def spread(v, t):
        rows = [jnp.broadcast_to(v[r : r + 1], (members, lanes)) for r in (t, t + 1)]
        return jnp.concatenate(rows, axis=0)

    for p in range(tiles // 2):
        w8, l8, t8 = spread(weight, 2 * p), spread(live, 2 * p), spread(limit, 2 * p)

        def keep(first, v):
            high = v.astype(jnp.bfloat16)
            low = (v - high.astype(jnp.float32)).astype(jnp.bfloat16)
            left_ref[first : first + v.shape[0], p * lanes : (p + 1) * lanes] = high
            left_ref[first : first + v.shape[0], width + p * lanes : width + (p + 1) * lanes] = low

        for d in range(0, days_in, CHUNK):
            n = min(CHUNK, days_in - d)
            e = jnp.maximum(x_ref[d : d + n, p * group : (p + 1) * group, :] - t8[None], 0.0)
            excess_ref[d : d + n, p * group : (p + 1) * group, :] = e
            rows = (e * w8[None]).reshape(n * group, lanes)
            if d + n == days_in:
                rows = jnp.concatenate([rows, w8, l8, jnp.zeros((left_ref.shape[0] - (days_in + 2) * group, lanes), jnp.float32)], axis=0)
            keep(d * group, rows)


def cell_sums(step, excess_ref, live, outs, total_ref):
    days_in = excess_ref.shape[0]
    tiles, lanes = live.shape
    members = excess_ref.shape[1] // tiles
    block_days = outs[0].shape[0]
    for d in range(0, days_in, CHUNK):
        n = min(CHUNK, days_in - d)
        total = excess_ref[d : d + n, pl.ds(0, tiles, stride=members), :]
        for m in range(1, members):
            total = total + excess_ref[d : d + n, pl.ds(m, tiles, stride=members), :]
        total_ref[d : d + n] = total
    me = lax.axis_index("x")
    scale = live * (1.0 / (WINDOW * members * PARTS))
    early = (2 * step < pl.num_programs(0)).astype(jnp.int32)
    ahead = (0, 1 + early, 2 + early, 3 - 2 * early)
    for k, out in zip(ahead, outs):
        first = lax.rem(me + k, PARTS) * block_days
        s = total_ref[pl.ds(first, block_days + WINDOW - 1)]
        pair = s[:-1] + s[1:]
        rolled = pair[0:block_days] + pair[2 : 2 + block_days] + pair[4 : 4 + block_days]
        out[...] = rolled * scale[None]


def region_sums(step, left_ref, rid_ref, acc_ref):
    tiles, lanes = rid_ref.shape
    region = lax.broadcasted_iota(jnp.int32, (HALF, lanes), 0)

    def hot(t):
        return (region == rid_ref[t : t + 1, :]).astype(jnp.float32)

    even = jnp.concatenate([hot(t) for t in range(0, tiles, 2)], axis=1)
    odd = jnp.concatenate([hot(t) for t in range(1, tiles, 2)], axis=1)
    right = jnp.concatenate([even, odd], axis=0).astype(jnp.bfloat16)
    right = jnp.concatenate([right, right], axis=1)
    part = lax.dot_general(
        left_ref[...], right, (((1,), (1,)), ((), ())), preferred_element_type=jnp.float32
    )

    @pl.when(step == 0)
    def _():
        acc_ref[...] = part

    @pl.when(step > 0)
    def _():
        acc_ref[...] += part


def packed_sums(acc_ref, sums_ref, days_in, members):
    group = 2 * members
    days = days_in - WINDOW + 1
    columns = sums_ref.shape[1] // members
    v = acc_ref[: (days_in + 2) * group].reshape(days_in + 2, group, 2 * HALF)
    pair = v[: days_in - 1] + v[1:days_in]
    rolled = (pair[0:days] + pair[2 : 2 + days] + pair[4 : 4 + days]) * (1.0 / WINDOW)
    acc_ref[: days * group] = rolled.reshape(days * group, 2 * HALF)
    acc_ref[days * group : (days + 2) * group] = v[days_in:].reshape(2 * group, 2 * HALF)
    rows = []
    for m in range(members):
        even = acc_ref[pl.ds(m, columns, stride=group), :]
        odd = acc_ref[pl.ds(members + m, columns, stride=group), :]
        rows.append(even + pltpu.roll(odd, HALF, 1))
    sums_ref[...] = jnp.concatenate(rows, axis=0).T[: sums_ref.shape[0]]


def fold_kernel(fill_ref, x_ref, thr_ref, mask_ref, rid_ref, area_ref, *refs):
    *outs, sums_ref, acc_ref, total_ref, excess_ref, left_ref = refs
    step = pl.program_id(0)
    live = live_cells(fill_ref, mask_ref, step)
    limit = thr_ref[...].astype(jnp.float32) * 0.1
    excess_terms(x_ref, area_ref[...] * live, live, limit, excess_ref, left_ref)
    region_sums(step, left_ref, rid_ref, acc_ref)
    cell_sums(step, excess_ref, live, outs, total_ref)

    @pl.when(step == pl.num_programs(0) - 1)
    def _():
        packed_sums(acc_ref, sums_ref, x_ref.shape[0], x_ref.shape[1] // live.shape[0])


def last_kernel(
    mine_ref, other_ref, own_ref, below_ref, above_ref, far_ref, near_ref,
    index_ref, count_ref, mean_ref, total_ref,
):
    block_days, tiles, lanes = own_ref.shape
    cut = tiles // 2
    first = own_ref[:, :cut] + above_ref[:, :cut] + near_ref[...]
    second = own_ref[:, cut:] + below_ref[:, cut:] + far_ref[...]
    total_ref[: block_days * cut] = first.reshape(block_days * cut, lanes)
    total_ref[block_days * cut :] = second.reshape(block_days * cut, lanes)
    for t in range(tiles):
        rows = pl.ds(t // cut * block_days * cut + t % cut, block_days, stride=cut)
        mean_ref[:, t * lanes : (t + 1) * lanes] = total_ref[rows, :]
    region_table(mine_ref, other_ref, index_ref, count_ref)


def region_table(mine_ref, other_ref, index_ref, count_ref):
    members, days = index_ref.shape[1:]
    width = mine_ref.shape[1]
    columns = width // members
    first = lax.axis_index("core") == 0
    mine, other = mine_ref[...], other_ref[...]
    table = jnp.concatenate([jnp.where(first, mine, other), jnp.where(first, other, mine)], axis=0)
    count = jnp.broadcast_to(table[:, days + 1 : days + 2], (table.shape[0], 128)).T
    count_ref[...] = count[:1, :REGIONS].astype(jnp.int32)
    table = table / table[:, days : days + 1]
    for m in range(members):
        shifted = pltpu.roll(table, (width - m * columns) % width, 1) if m else table
        index_ref[:, m, :] = shifted[:REGIONS, :days]


def call(kernel, fill, x, flats, blocks, regional):
    days_in, rows, lanes = x.shape
    tiles = flats[0].shape[0]
    members = rows // tiles
    block_days = (days_in - WINDOW + 1) // PARTS
    flat = pl.BlockSpec((TILES, lanes), lambda i: (i, 0))
    out_specs = [pl.BlockSpec((block_days, TILES, lanes), lambda i: (0, i, 0))] * blocks
    out_shape = [jax.ShapeDtypeStruct((block_days, tiles, lanes), jnp.float32)] * blocks
    scratch = []
    if regional:
        columns = -(-(days_in - WINDOW + 3) // 8) * 8
        sums = (ROWS, members * columns)
        out_specs.append(pl.BlockSpec(sums, lambda i: (0, 0)))
        out_shape.append(jax.ShapeDtypeStruct(sums, jnp.float32))
        high = -(-(days_in + 2) * 2 * members // 16) * 16
        scratch = [
            pltpu.VMEM((high, 2 * HALF), jnp.float32),
            pltpu.VMEM((days_in, TILES, lanes), jnp.float32),
            pltpu.VMEM((days_in, TILES * members, lanes), jnp.float32),
            pltpu.VMEM((high, TILES * lanes), jnp.bfloat16),
        ]
    return pl.pallas_call(
        kernel,
        grid=(tiles // TILES,),
        in_specs=[
            pl.BlockSpec(fill.shape, lambda i: (0, 0)),
            pl.BlockSpec((days_in, TILES * members, lanes), lambda i: (0, i, 0)),
        ]
        + [flat] * len(flats),
        out_specs=out_specs,
        out_shape=out_shape,
        scratch_shapes=scratch,
        compiler_params=pltpu.CompilerParams(vmem_limit_bytes=40 * 1024 * 1024),
    )(*[pltpu.with_memory_space_constraint(a, pltpu.HBM) for a in (fill, x, *flats)])


def moved(array, axis, shift):
    size = lax.axis_size(axis)
    return lax.ppermute(array, axis, [(i, (i + shift) % size) for i in range(size)])


def sum_over_cells(sums):
    core = lax.axis_index("core")
    halves = sums.reshape(2, -1, *sums.shape[1:])
    mine = lax.dynamic_index_in_dim(halves, core, 0, False)
    other = lax.dynamic_index_in_dim(halves, 1 - core, 0, False)
    mine = mine + moved(other, "core", 1)
    mine = mine + moved(mine, "y", 1) + moved(mine, "y", 2) + moved(mine, "y", 3)
    two = mine + moved(mine, "z", 7)
    three = two + moved(mine, "z", 1)
    mine = three + moved(three, "z", 5) + moved(two, "z", 3)
    return mine, moved(mine, "core", 1)


def sum_over_members(own, up, down, late):
    cut = own.shape[1] // 2
    from_below, from_above = moved(up, "x", 1), moved(down, "x", 3)
    near = moved(late[:, :cut] + from_below[:, :cut], "x", 1)
    far = moved(late[:, cut:] + from_above[:, cut:], "x", 3)
    return own, from_below, from_above, far, near


def shards(tmax, threshold, land_mask, region_id, block_fill, cell_area):
    members, days_in, cells = tmax.shape
    blocks = block_fill.shape[0]
    lanes = cells // blocks
    days = days_in - WINDOW + 1
    x = tmax.reshape(members, days_in, blocks, lanes).transpose(1, 2, 0, 3)
    x = x.reshape(days_in, blocks * members, lanes)
    threshold, land_mask, region_id, cell_area = (
        a.reshape(blocks, lanes) for a in (threshold, land_mask, region_id, cell_area)
    )
    *terms, sums = call(
        fold_kernel, block_fill.reshape(1, blocks), x, (threshold, land_mask, region_id, cell_area), PARTS, True
    )
    terms = sum_over_members(*terms)
    mine, other = sum_over_cells(sums)
    block_days = terms[0].shape[0]
    region_index, land_count, cell_mean = pl.pallas_call(
        last_kernel,
        out_shape=[
            jax.ShapeDtypeStruct((REGIONS, members, days), jnp.float32),
            jax.ShapeDtypeStruct((1, REGIONS), jnp.int32),
            jax.ShapeDtypeStruct((block_days, cells), jnp.float32),
        ],
        scratch_shapes=[pltpu.VMEM((block_days * blocks, lanes), jnp.float32)],
        compiler_params=pltpu.CompilerParams(vmem_limit_bytes=8 * 1024 * 1024),
    )(mine, other, *terms)
    return region_index.transpose(1, 2, 0), cell_mean, land_count.reshape(REGIONS)


def solution(mesh):
    devices = mesh.devices.reshape(4, 8, 2, 4)
    fine = Mesh(devices, ("y", "z", "core", "x"))
    cells = P(CELL_AXES)
    return jax.shard_map(
        shards,
        mesh=fine,
        in_specs=(P("x", None, CELL_AXES), cells, cells, cells, cells, cells),
        out_specs=(P("x", None, None), P("x", CELL_AXES), P()),
        check_vma=False,
    )
```

```python
import jax
import jax.numpy as jnp
from jax import lax
from jax.experimental import pallas as pl
from jax.experimental.pallas import tpu as pltpu
from jax.sharding import Mesh, PartitionSpec as P

WINDOW = 6
REGIONS = 46
HALF = 64
PARTS = 4
ROWS = 48
TILES = 16
CHUNK = 8
CELL_AXES = ("y", "z", "core")


def live_cells(fill_ref, mask_ref, step):
    tiles, lanes = mask_ref.shape
    blocks = fill_ref.shape[1]
    row = lax.broadcasted_iota(jnp.int32, (tiles, blocks), 0) + step * tiles
    here = row == lax.broadcasted_iota(jnp.int32, (tiles, blocks), 1)
    fill = jnp.where(here, fill_ref[...].astype(jnp.float32), 0.0)
    fill = jnp.sum(fill, axis=1, keepdims=True).astype(jnp.int32)
    lane = lax.broadcasted_iota(jnp.int32, (tiles, lanes), 1)
    return jnp.where(lane < fill, mask_ref[...], 0).astype(jnp.float32)


def excess_terms(x_ref, weight, live, limit, excess_ref, left_ref):
    days_in = x_ref.shape[0]
    tiles, lanes = live.shape
    members = x_ref.shape[1] // tiles
    group = 2 * members
    width = tiles // 2 * lanes

    def spread(v, t):
        rows = [jnp.broadcast_to(v[r : r + 1], (members, lanes)) for r in (t, t + 1)]
        return jnp.concatenate(rows, axis=0)

    for p in range(tiles // 2):
        w8, l8, t8 = spread(weight, 2 * p), spread(live, 2 * p), spread(limit, 2 * p)

        def keep(first, v):
            high = v.astype(jnp.bfloat16)
            low = (v - high.astype(jnp.float32)).astype(jnp.bfloat16)
            left_ref[first : first + v.shape[0], p * lanes : (p + 1) * lanes] = high
            left_ref[first : first + v.shape[0], width + p * lanes : width + (p + 1) * lanes] = low

        for d in range(0, days_in, CHUNK):
            n = min(CHUNK, days_in - d)
            e = jnp.maximum(x_ref[d : d + n, p * group : (p + 1) * group, :] - t8[None], 0.0)
            excess_ref[d : d + n, p * group : (p + 1) * group, :] = e
            rows = (e * w8[None]).reshape(n * group, lanes)
            if d + n == days_in:
                rows = jnp.concatenate([rows, w8, l8, jnp.zeros((left_ref.shape[0] - (days_in + 2) * group, lanes), jnp.float32)], axis=0)
            keep(d * group, rows)


def cell_sums(step, excess_ref, live, outs, total_ref):
    days_in = excess_ref.shape[0]
    tiles, lanes = live.shape
    members = excess_ref.shape[1] // tiles
    block_days = outs[0].shape[0]
    for d in range(0, days_in, CHUNK):
        n = min(CHUNK, days_in - d)
        total = excess_ref[d : d + n, pl.ds(0, tiles, stride=members), :]
        for m in range(1, members):
            total = total + excess_ref[d : d + n, pl.ds(m, tiles, stride=members), :]
        total_ref[d : d + n] = total
    me = lax.axis_index("x")
    scale = live * (1.0 / (WINDOW * members * PARTS))
    early = (2 * step < pl.num_programs(0)).astype(jnp.int32)
    ahead = (0, 1 + early, 2 + early, 3 - 2 * early)
    for k, out in zip(ahead, outs):
        first = lax.rem(me + k, PARTS) * block_days
        s = total_ref[pl.ds(first, block_days + WINDOW - 1)]
        pair = s[:-1] + s[1:]
        rolled = pair[0:block_days] + pair[2 : 2 + block_days] + pair[4 : 4 + block_days]
        out[...] = rolled * scale[None]


def region_sums(step, left_ref, rid_ref, acc_ref):
    tiles, lanes = rid_ref.shape
    region = lax.broadcasted_iota(jnp.int32, (HALF, lanes), 0)

    def hot(t):
        return (region == rid_ref[t : t + 1, :]).astype(jnp.float32)

    even = jnp.concatenate([hot(t) for t in range(0, tiles, 2)], axis=1)
    odd = jnp.concatenate([hot(t) for t in range(1, tiles, 2)], axis=1)
    right = jnp.concatenate([even, odd], axis=0).astype(jnp.bfloat16)
    right = jnp.concatenate([right, right], axis=1)
    part = lax.dot_general(
        left_ref[...], right, (((1,), (1,)), ((), ())), preferred_element_type=jnp.float32
    )

    @pl.when(step == 0)
    def _():
        acc_ref[...] = part

    @pl.when(step > 0)
    def _():
        acc_ref[...] += part


def packed_sums(acc_ref, sums_ref, days_in, members):
    group = 2 * members
    days = days_in - WINDOW + 1
    columns = sums_ref.shape[1] // members
    v = acc_ref[: (days_in + 2) * group].reshape(days_in + 2, group, 2 * HALF)
    pair = v[: days_in - 1] + v[1:days_in]
    rolled = (pair[0:days] + pair[2 : 2 + days] + pair[4 : 4 + days]) * (1.0 / WINDOW)
    acc_ref[: days * group] = rolled.reshape(days * group, 2 * HALF)
    acc_ref[days * group : (days + 2) * group] = v[days_in:].reshape(2 * group, 2 * HALF)
    rows = []
    for m in range(members):
        even = acc_ref[pl.ds(m, columns, stride=group), :]
        odd = acc_ref[pl.ds(members + m, columns, stride=group), :]
        rows.append(even + pltpu.roll(odd, HALF, 1))
    sums_ref[...] = jnp.concatenate(rows, axis=0).T[: sums_ref.shape[0]]


def fold_kernel(fill_ref, x_ref, thr_ref, mask_ref, rid_ref, area_ref, *refs):
    *outs, sums_ref, acc_ref, total_ref, excess_ref, left_ref = refs
    step = pl.program_id(0)
    live = live_cells(fill_ref, mask_ref, step)
    limit = thr_ref[...].astype(jnp.float32) * 0.1
    excess_terms(x_ref, area_ref[...] * live, live, limit, excess_ref, left_ref)
    region_sums(step, left_ref, rid_ref, acc_ref)
    cell_sums(step, excess_ref, live, outs, total_ref)

    @pl.when(step == pl.num_programs(0) - 1)
    def _():
        packed_sums(acc_ref, sums_ref, x_ref.shape[0], x_ref.shape[1] // live.shape[0])


def last_kernel(
    mine_ref, other_ref, own_ref, below_ref, above_ref, far_ref, near_ref,
    index_ref, count_ref, mean_ref, total_ref,
):
    block_days, tiles, lanes = own_ref.shape
    cut = tiles // 2
    first = own_ref[:, :cut] + above_ref[:, :cut] + near_ref[...]
    second = own_ref[:, cut:] + below_ref[:, cut:] + far_ref[...]
    total_ref[: block_days * cut] = first.reshape(block_days * cut, lanes)
    total_ref[block_days * cut :] = second.reshape(block_days * cut, lanes)
    for t in range(tiles):
        rows = pl.ds(t // cut * block_days * cut + t % cut, block_days, stride=cut)
        mean_ref[:, t * lanes : (t + 1) * lanes] = total_ref[rows, :]
    region_table(mine_ref, other_ref, index_ref, count_ref)


def region_table(mine_ref, other_ref, index_ref, count_ref):
    members, days = index_ref.shape[1:]
    width = mine_ref.shape[1]
    columns = width // members
    first = lax.axis_index("core") == 0
    mine, other = mine_ref[...], other_ref[...]
    table = jnp.concatenate([jnp.where(first, mine, other), jnp.where(first, other, mine)], axis=0)
    count = jnp.broadcast_to(table[:, days + 1 : days + 2], (table.shape[0], 128)).T
    count_ref[...] = count[:1, :REGIONS].astype(jnp.int32)
    table = table / table[:, days : days + 1]
    for m in range(members):
        shifted = pltpu.roll(table, (width - m * columns) % width, 1) if m else table
        index_ref[:, m, :] = shifted[:REGIONS, :days]


def call(kernel, fill, x, flats, blocks, regional):
    days_in, rows, lanes = x.shape
    tiles = flats[0].shape[0]
    members = rows // tiles
    block_days = (days_in - WINDOW + 1) // PARTS
    flat = pl.BlockSpec((TILES, lanes), lambda i: (i, 0))
    out_specs = [pl.BlockSpec((block_days, TILES, lanes), lambda i: (0, i, 0))] * blocks
    out_shape = [jax.ShapeDtypeStruct((block_days, tiles, lanes), jnp.float32)] * blocks
    scratch = []
    if regional:
        columns = -(-(days_in - WINDOW + 3) // 8) * 8
        sums = (ROWS, members * columns)
        out_specs.append(pl.BlockSpec(sums, lambda i: (0, 0)))
        out_shape.append(jax.ShapeDtypeStruct(sums, jnp.float32))
        high = -(-(days_in + 2) * 2 * members // 16) * 16
        scratch = [
            pltpu.VMEM((high, 2 * HALF), jnp.float32),
            pltpu.VMEM((days_in, TILES, lanes), jnp.float32),
            pltpu.VMEM((days_in, TILES * members, lanes), jnp.float32),
            pltpu.VMEM((high, TILES * lanes), jnp.bfloat16),
        ]
    return pl.pallas_call(
        kernel,
        grid=(tiles // TILES,),
        in_specs=[
            pl.BlockSpec(fill.shape, lambda i: (0, 0)),
            pl.BlockSpec((days_in, TILES * members, lanes), lambda i: (0, i, 0)),
        ]
        + [flat] * len(flats),
        out_specs=out_specs,
        out_shape=out_shape,
        scratch_shapes=scratch,
        compiler_params=pltpu.CompilerParams(vmem_limit_bytes=40 * 1024 * 1024),
    )(*[pltpu.with_memory_space_constraint(a, pltpu.HBM) for a in (fill, x, *flats)])


def moved(array, axis, shift):
    size = lax.axis_size(axis)
    return lax.ppermute(array, axis, [(i, (i + shift) % size) for i in range(size)])


def sum_over_cells(sums):
    core = lax.axis_index("core")
    halves = sums.reshape(2, -1, *sums.shape[1:])
    mine = lax.dynamic_index_in_dim(halves, core, 0, False)
    other = lax.dynamic_index_in_dim(halves, 1 - core, 0, False)
    mine = mine + moved(other, "core", 1)
    mine = mine + moved(mine, "y", 1) + moved(mine, "y", 3) + moved(mine, "y", 2)
    two = mine + moved(mine, "z", 7)
    three = two + moved(mine, "z", 1)
    mine = three + moved(three, "z", 5) + moved(two, "z", 3)
    return mine, moved(mine, "core", 1)


def sum_over_members(own, up, down, late):
    cut = own.shape[1] // 2
    from_below, from_above = moved(up, "x", 1), moved(down, "x", 3)
    near = moved(late[:, :cut] + from_below[:, :cut], "x", 1)
    far = moved(late[:, cut:] + from_above[:, cut:], "x", 3)
    return own, from_below, from_above, far, near


def shards(tmax, threshold, land_mask, region_id, block_fill, cell_area):
    members, days_in, cells = tmax.shape
    blocks = block_fill.shape[0]
    lanes = cells // blocks
    days = days_in - WINDOW + 1
    x = tmax.reshape(members, days_in, blocks, lanes).transpose(1, 2, 0, 3)
    x = x.reshape(days_in, blocks * members, lanes)
    threshold, land_mask, region_id, cell_area = (
        a.reshape(blocks, lanes) for a in (threshold, land_mask, region_id, cell_area)
    )
    *terms, sums = call(
        fold_kernel, block_fill.reshape(1, blocks), x, (threshold, land_mask, region_id, cell_area), PARTS, True
    )
    terms = sum_over_members(*terms)
    mine, other = sum_over_cells(sums)
    block_days = terms[0].shape[0]
    region_index, land_count, cell_mean = pl.pallas_call(
        last_kernel,
        out_shape=[
            jax.ShapeDtypeStruct((REGIONS, members, days), jnp.float32),
            jax.ShapeDtypeStruct((1, REGIONS), jnp.int32),
            jax.ShapeDtypeStruct((block_days, cells), jnp.float32),
        ],
        scratch_shapes=[pltpu.VMEM((block_days * blocks, lanes), jnp.float32)],
        compiler_params=pltpu.CompilerParams(vmem_limit_bytes=8 * 1024 * 1024),
    )(mine, other, *terms)
    return region_index.transpose(1, 2, 0), cell_mean, land_count.reshape(REGIONS)


def solution(mesh):
    devices = mesh.devices.reshape(4, 8, 2, 4)
    fine = Mesh(devices, ("y", "z", "core", "x"))
    cells = P(CELL_AXES)
    return jax.shard_map(
        shards,
        mesh=fine,
        in_specs=(P("x", None, CELL_AXES), cells, cells, cells, cells, cells),
        out_specs=(P("x", None, None), P("x", CELL_AXES), P()),
        check_vma=False,
    )
```
